256 devices in a mesh: dp: 16 (over z, core), blk: 16 (over y, x).
Axes of the slice: x: 4, y: 4, z: 8, core: 2. Of those that a mesh axis runs over, the one named last changes fastest.
Arguments:
- frames: bfloat16 [64, 1280, 256], P('dp', 'blk'), may hold values from -6 to 6
- weight: bfloat16 [1280, 11520], P('blk'), may hold values from -0.0546875 to 0.0546875
- bias: float32 [1280], P('blk'), may hold values from -3 to 3
- cotangent: bfloat16 [64, 1280, 256], P('dp', 'blk'), may hold values from -6 to 6
Outputs:
- response: bfloat16 [64, 1280, 256], P('dp', 'blk')
- frame_grad: bfloat16 [64, 1280, 256], P('dp', 'blk')
- weight_grad: float32 [1280, 11520], P(('blk', 'dp'))
The draws below stay inside these ranges and needn't reach their ends.
All inputs are finite; a program needn't handle non-finite values.
Results may differ from the reference program's by a relative error of at most 0.001.
Values may be sent and summed in bfloat16 or wider, within the bound.
A program may use at most 128 MiB of HBM per device.

```python
import jax
import jax.numpy as jnp
from jax import lax

C = 1280
H = 16
WD = 16
FRAMES = 64


def strengthened(result, stream_key, source, target, parts, factor):
    def block_of(axis_at):
        return (jnp.arange(result.shape[axis_at]) // (result.shape[axis_at] // parts)).reshape((-1,) + (1,) * (result.ndim - 1 - axis_at))

    one_side = jax.random.permutation(stream_key, parts)[block_of(target)]
    other_side = (block_of(target) + parts // 2) % parts
    return jnp.where((block_of(source) == one_side) | (block_of(source) == other_side), factor * result, result)


def levels(key, shape, shards, least, largest):
    factor_of, own = 1.0, jax.random.fold_in(key, 6)
    for dim, parts in shards:
        draws = jnp.exp(jax.random.uniform(jax.random.fold_in(own, dim), (parts,), jnp.float32, least / len(shards), largest / len(shards)))
        factor_of = factor_of * jnp.repeat(draws, shape[dim] // parts).reshape([-1 if axis == dim else 1 for axis in range(len(shape))])
    return factor_of


def bell_draw(own_key, shape, width, bound, cuts=(), held_as=jnp.bfloat16):
    loudness = levels(own_key, shape, cuts, -0.22, 0.18) if cuts else 1.0
    values = jax.random.normal(own_key, shape, jnp.float32) * width * loudness
    return jnp.minimum(jnp.maximum(values, -bound), bound).astype(held_as)


def bell_draw_with(rng, extent, width, limit, cuts, heavy, held_as=jnp.bfloat16):
    result = width * jax.random.normal(rng, extent, jnp.float32)
    if cuts:
        result = result * levels(rng, extent, cuts, -0.22, 0.18)
    return jnp.clip(strengthened(result, jax.random.fold_in(rng, 3), *heavy), -limit, limit).astype(held_as)


def setup_inputs(seed: int = 0) -> dict:
    seeds = jax.random.split(jax.random.key(seed), 5)
    frames = bell_draw_with(seeds[0], (FRAMES, C, H * WD), 1.0, 6.0, ((0, 16), (1, 16)), (0, 1, 16, 2.0))
    weight = bell_draw(seeds[1], (C, 9 * C), (9 * C) ** -0.5, 0.0546875, ((0, 16),))
    bias = bell_draw(seeds[2], (C,), 0.5, 3.0, ((0, 16),), jnp.float32)
    cotangent = bell_draw(seeds[3], (FRAMES, C, H * WD), 1.0, 6.0, ((0, 16), (1, 16)))
    return {"frames": frames, "weight": weight, "bias": bias, "cotangent": cotangent}


def reference(frames, weight, bias, cotangent):
    nf, chans, cells = frames.shape
    rows = cells // WD
    cols = WD
    maps = jnp.transpose(frames.reshape(nf, chans, rows, cols), (0, 2, 3, 1))
    cot_maps = jnp.transpose(cotangent.reshape(nf, chans, rows, cols), (0, 2, 3, 1))
    padded = jnp.pad(maps, ((0, 0), (1, 1), (1, 1), (0, 0)))
    cot_padded = jnp.pad(cot_maps, ((0, 0), (1, 1), (1, 1), (0, 0)))
    cot_flat = cot_maps.reshape(-1, chans)
    total = jnp.zeros((nf * rows * cols, chans), jnp.float32)
    back = jnp.zeros((nf * rows * cols, chans), jnp.float32)
    grads = []
    for tap in range(9):
        ky, kx = divmod(tap, 3)
        w_tap = weight[:, tap * chans:(tap + 1) * chans]
        piece = padded[:, ky:ky + rows, kx:kx + cols, :].reshape(-1, chans)
        total = total + jnp.dot(piece, w_tap.T, preferred_element_type=jnp.float32)
        grads.append(lax.dot_general(cot_flat, piece, (((0,), (0,)), ((), ())), preferred_element_type=jnp.float32))
        cpiece = cot_padded[:, 2 - ky:2 - ky + rows, 2 - kx:2 - kx + cols, :].reshape(-1, chans)
        back = back + jnp.dot(cpiece, w_tap, preferred_element_type=jnp.float32)
    total = total + bias[None, :]
    response = jnp.transpose(total.reshape(nf, cells, chans), (0, 2, 1)).astype(jnp.bfloat16)
    frame_grad = jnp.transpose(back.reshape(nf, cells, chans), (0, 2, 1)).astype(jnp.bfloat16)
    weight_grad = jnp.concatenate(grads, axis=1)
    return response, frame_grad, weight_grad
```

```python
import functools

import jax
import jax.numpy as jnp
import ml_dtypes
import numpy as np
from jax import lax
from jax.experimental import pallas as pl
from jax.experimental.pallas import tpu as pltpu
from jax.sharding import PartitionSpec as P

MESH = pl.DeviceIdType.MESH
CH = 80
NB = 16
C = CH * NB
TAPS = 9
CELLS = 256
NF = 4
PAD = 768
HALF = 384
ROWS = 48
NQ = 5

RELAYS = [(1, 0), (3, 0), (0, 1), (2, 0), (1, 1), (3, 1), (2, 1)]
LEAVES = [(0, 3), (1, 3), (3, 3), (2, 3), (0, 2), (1, 2), (3, 2), (2, 2)]
TREES = [(True, 1), (True, -1), (False, 1), (False, -1)]


def offsets(tap):
    return tap // 3 - 1, tap % 3 - 1


def moved(v, dy, dx):
    if dy == 0 and dx == 0:
        return v
    cell = lax.broadcasted_iota(jnp.int32, (1, CELLS), 1)
    h = lax.shift_right_logical(cell, 4) + dy
    w = lax.bitwise_and(cell, 15) + dx
    keep = (h >= 0) & (h < 16) & (w >= 0) & (w < 16)
    rolled = pltpu.roll(v, (-(dy * 16 + dx)) % CELLS, axis=1)
    return jnp.where(keep, rolled, jnp.zeros_like(rolled))


def kernel(nz, frames_hbm, weight_hbm, bias_ref, cot_hbm, perm_ref,
           resp_ref, fgrad_ref, wgrad_ref,
           g, ws, pb, r, rt, cst, csp, pw, mb, s, rp,
           lsem, wlsem, ag_s, ag_r, w_s, w_r, d_s, d_r, m_s, m_r, rs_s, rs_r):
    dp = lax.axis_index("dp")
    blk = lax.axis_index("blk")
    z, core = dp // 2, lax.rem(dp, 2)
    y, x = blk // 4, lax.rem(blk, 4)
    sib = (z * 2 + 1 - core, blk)

    def plane(b):
        return (dp, b)

    def zdev(step):
        return (lax.rem(z + step + nz, nz) * 2 + core, blk)

    loads = []
    for a, src in enumerate((frames_hbm, cot_hbm)):
        for f in range(NF):
            cp = pltpu.make_async_copy(
                src.at[f], g.at[a, f, pl.ds(pl.multiple_of(blk * CH, 16), CH), :], lsem.at[a, f])
            cp.start()
            loads.append(cp)
    wloads = []
    for t in range(TAPS):
        cp = pltpu.make_async_copy(
            weight_hbm.at[:, pl.ds(t * C, C)], ws.at[pl.ds(t * CH, CH), :], wlsem.at[t])
        cp.start()
        wloads.append(cp)

    barrier = pltpu.get_barrier_semaphore()
    for k in range(1, NB):
        pl.semaphore_signal(barrier, inc=1, device_id=plane(lax.rem(blk + k, NB)), device_id_type=MESH)
    for dev in (sib, zdev(1), zdev(-1)):
        pl.semaphore_signal(barrier, inc=1, device_id=dev, device_id_type=MESH)
    for cp in loads:
        cp.wait()
    pl.semaphore_wait(barrier, NB + 2)

    pending = []

    def remote(src, dst, ssem, rsem, dev):
        cp = pltpu.make_async_remote_copy(
            src_ref=src, dst_ref=dst, send_sem=ssem, recv_sem=rsem,
            device_id=dev, device_id_type=MESH)
        cp.start()
        pending.append(cp)

    def at(tree, step_a, step_b):
        first_x, _ = TREES[tree]
        sx, sy = (step_a, step_b) if first_x else (step_b, step_a)
        return lax.rem(y + sy + 4, 4) * 4 + lax.rem(x + sx + 4, 4)

    def block(a, f, ra, rb):
        sgn = TREES[f][1]
        src = at(f, -sgn * (ra if ra < 3 else -1), -sgn * (rb if rb < 3 else -1))
        return g.at[a, f, pl.ds(pl.multiple_of(src * CH, 16), CH), :]

    counts = {}

    def push(a, f, ra, rb, along_a, forward):
        n = counts.get((a, f), 0)
        counts[(a, f)] = n + 1
        sgn = TREES[f][1]
        step = sgn if forward else -sgn
        dev = at(f, step, 0) if along_a else at(f, 0, step)
        if along_a:
            there = (ra + 1 if forward else 3, rb)
        else:
            there = (ra, rb + 1 if forward else 3)
        ref = block(a, f, ra, rb)
        remote(ref, ref, ag_s.at[a, f, n], ag_r.at[a, f, there[0] * 4 + there[1]], plane(dev))

    def arrived(a, f, ra, rb):
        ref = block(a, f, ra, rb)
        pltpu.make_async_remote_copy(
            src_ref=ref, dst_ref=ref, send_sem=ag_s.at[a, f, 0],
            recv_sem=ag_r.at[a, f, ra * 4 + rb], device_id=plane(at(f, 1, 0)),
            device_id_type=MESH).wait_recv()

    def own_sends(a):
        for f in range(NF):
            push(a, f, 0, 0, True, True)
            push(a, f, 0, 0, False, True)
            push(a, f, 0, 0, True, False)
            push(a, f, 0, 0, False, False)

    def relay(a, event):
        ra, rb = event
        for f in range(NF):
            arrived(a, f, ra, rb)
            if rb == 0:
                if ra == 1:
                    push(a, f, ra, rb, True, True)
                push(a, f, ra, rb, False, True)
                push(a, f, ra, rb, False, False)
            elif rb == 1:
                push(a, f, ra, rb, False, True)

    def leaves(a, event):
        for f in range(NF):
            arrived(a, f, *event)

    own_sends(0)

    for cp in wloads:
        cp.wait()

    def pack(half):
        for b in range(NB):
            parts = []
            for t in range(TAPS):
                lo, hi = max(t * CH, half * HALF), min((t + 1) * CH, (half + 1) * HALF)
                if lo < hi:
                    parts.append(ws[t * CH:(t + 1) * CH, b * CH + lo - t * CH:b * CH + hi - t * CH])
            if half == 1:
                parts.append(jnp.zeros((CH, PAD - TAPS * CH), jnp.bfloat16))
            pb[b] = jnp.concatenate(parts, axis=1)

    @pl.when(core == 0)
    def _():
        pack(0)

    @pl.when(core == 1)
    def _():
        pack(1)

    mine = pl.ds(pl.multiple_of(blk * CH, 16), CH)
    own_w = pltpu.make_async_copy(pb.at[blk], r.at[core, mine, :], w_s.at[0])
    own_w.start()
    for k in range(1, NB):
        b = lax.rem(blk + k, NB)
        remote(pb.at[b], r.at[core, mine, :], w_s.at[k], w_r.at[k], plane(b))

    relay(0, RELAYS[0])
    relay(0, RELAYS[1])
    relay(0, RELAYS[2])
    relay(0, RELAYS[3])

    def shifted(f):
        cot = g[1, f, mine, :].astype(jnp.float32)
        for t in range(TAPS):
            dy, dx = offsets(t)
            cst[t * CH:(t + 1) * CH, :] = moved(cot, -dy, -dx).astype(jnp.bfloat16)
        csp[:, f * CELLS:(f + 1) * CELLS] = jnp.dot(
            perm_ref[...], cst[...], preferred_element_type=jnp.float32).astype(jnp.bfloat16)

    shifted(0)
    relay(0, RELAYS[4])
    shifted(1)
    relay(0, RELAYS[5])
    shifted(2)
    relay(0, RELAYS[6])
    own_sends(1)
    shifted(3)
    for ev in LEAVES:
        leaves(0, ev)
    relay(1, RELAYS[0])
    relay(1, RELAYS[1])

    for q in range(NQ):
        acc = None
        for f in range(NF):
            part = lax.dot_general(
                csp[:, f * CELLS:(f + 1) * CELLS], g[0, f, q * 256:(q + 1) * 256, :],
                (((1,), (1,)), ((), ())), preferred_element_type=jnp.float32)
            acc = part if acc is None else acc + part
        for c in range(2):
            pw[c, q] = acc[c * nz * ROWS:(c + 1) * nz * ROWS].reshape(nz, ROWS, 256)
        remote(pw.at[1 - core, q], mb.at[q], m_s.at[q], m_r.at[q], sib)
        relay(1, RELAYS[2 + q])

    def hops(q, forward):
        return 4 if (q % 2 == 0) == forward else 3

    def rs_send(q, forward, k):
        n = hops(q, forward)
        i = 0 if forward else 1
        dist = n - k
        to = lax.rem(z + dist, nz) if forward else lax.rem(z - dist + nz, nz)
        if k > 0:
            rs_wait(q, forward, k - 1)
            s[q, to] = s[q, to] + rp[i, q, k - 1]
        remote(s.at[q, to], rp.at[i, q, k], rs_s.at[i, q, k], rs_r.at[i, q, k],
               zdev(1 if forward else -1))

    def rs_wait(q, forward, k):
        i = 0 if forward else 1
        ref = rp.at[i, q, k]
        pltpu.make_async_remote_copy(
            src_ref=ref, dst_ref=ref, send_sem=rs_s.at[i, q, k], recv_sem=rs_r.at[i, q, k],
            device_id=zdev(1), device_id_type=MESH).wait_recv()

    for q in range(NQ):
        pltpu.make_async_remote_copy(
            src_ref=mb.at[q], dst_ref=mb.at[q], send_sem=m_s.at[q], recv_sem=m_r.at[q],
            device_id=sib, device_id_type=MESH).wait_recv()
        for k in range(nz):
            s[q, k] = pw[core, q, k] + mb[q, k]
        rs_send(q, True, 0)
        rs_send(q, False, 0)

    def forward_conv(a, f, lhs, sign):
        prod = jnp.dot(lhs[0:TAPS * CH, :], g[a, f], preferred_element_type=jnp.float32)
        total = None
        for t in range(TAPS):
            dy, dx = offsets(t)
            term = moved(prod[t * CH:(t + 1) * CH], sign * dy, sign * dx)
            total = term if total is None else total + term
        return total

    def respond(f):
        resp_ref[f] = (forward_conv(0, f, ws, 1) + bias_ref[...]).astype(jnp.bfloat16)

    def rs_round(k):
        for q in range(NQ):
            for forward in (True, False):
                if k < hops(q, forward):
                    rs_send(q, forward, k)

    for f in range(NF):
        respond(f)
        if f == 1:
            rs_round(1)
    for ev in LEAVES:
        leaves(1, ev)
    rs_round(2)

    own_w.wait()
    for k in range(1, NB):
        pltpu.make_async_remote_copy(
            src_ref=pb.at[0], dst_ref=r.at[core, pl.ds(0, CH), :], send_sem=w_s.at[k],
            recv_sem=w_r.at[k], device_id=sib, device_id_type=MESH).wait_recv()
    remote(r.at[core], r.at[core], d_s.at[0], d_r.at[0], sib)

    def turn(half):
        rt[pl.ds(pl.multiple_of(half * HALF, 128), HALF), :] = r[half].T

    turn(core)
    pltpu.make_async_remote_copy(
        src_ref=r.at[1 - core], dst_ref=r.at[1 - core], send_sem=d_s.at[0], recv_sem=d_r.at[0],
        device_id=sib, device_id_type=MESH).wait_recv()
    turn(1 - core)

    for f in range(NF):
        fgrad_ref[f] = forward_conv(1, f, rt, -1).astype(jnp.bfloat16)
        if f == 0:
            rs_round(3)

    for q in range(NQ):
        rs_wait(q, True, hops(q, True) - 1)
        rs_wait(q, False, hops(q, False) - 1)
        final = s[q, z] + rp[0, q, hops(q, True) - 1] + rp[1, q, hops(q, False) - 1]
        for t in range(TAPS):
            wgrad_ref[:, t * C + q * 256:t * C + (q + 1) * 256] = final[t * 5:(t + 1) * 5]

    for cp in pending:
        cp.wait_send()


def solution(mesh):
    nz = mesh.shape["dp"] // 2
    table = np.zeros((PAD, TAPS * CH), np.float32)
    for c in range(2):
        for k in range(nz):
            for t in range(TAPS):
                for j in range(5):
                    table[c * nz * ROWS + k * ROWS + t * 5 + j, t * CH + k * 10 + c * 5 + j] = 1
    table = table.astype(ml_dtypes.bfloat16)

    bf16, f32 = jnp.bfloat16, jnp.float32
    vmem = pl.BlockSpec(memory_space=pltpu.VMEM)
    hbm = pl.BlockSpec(memory_space=pl.ANY)
    dma = pltpu.SemaphoreType.DMA

    def body(frames, weight, bias, cotangent):
        return pl.pallas_call(
            functools.partial(kernel, nz),
            out_shape=(
                jax.ShapeDtypeStruct((NF, CH, CELLS), bf16),
                jax.ShapeDtypeStruct((NF, CH, CELLS), bf16),
                jax.ShapeDtypeStruct((5, TAPS * C), f32),
            ),
            in_specs=[hbm, hbm, vmem, hbm, vmem],
            out_specs=(vmem, vmem, vmem),
            scratch_shapes=[
                pltpu.VMEM((2, NF, C, CELLS), bf16),
                pltpu.VMEM((TAPS * CH, C), bf16),
                pltpu.VMEM((NB, CH, HALF), bf16),
                pltpu.VMEM((2, C, HALF), bf16),
                pltpu.VMEM((PAD, C), bf16),
                pltpu.VMEM((TAPS * CH, CELLS), bf16),
                pltpu.VMEM((PAD, NF * CELLS), bf16),
                pltpu.VMEM((2, NQ, nz, ROWS, 256), f32),
                pltpu.VMEM((NQ, nz, ROWS, 256), f32),
                pltpu.VMEM((NQ, nz, ROWS, 256), f32),
                pltpu.VMEM((2, NQ, 4, ROWS, 256), f32),
                dma((2, NF)), dma((TAPS,)),
                dma((2, NF, 15)), dma((2, NF, 16)),
                dma((NB,)), dma((NB,)),
                dma((1,)), dma((1,)),
                dma((NQ,)), dma((NQ,)),
                dma((2, NQ, 4)), dma((2, NQ, 4)),
            ],
            compiler_params=pltpu.CompilerParams(
                collective_id=0, has_side_effects=True, vmem_limit_bytes=60 * 1024 * 1024),
        )(frames, weight, bias[:, None], cotangent, jnp.asarray(table))

    return jax.shard_map(
        body,
        mesh=mesh,
        in_specs=(P("dp", "blk", None), P("blk", None), P("blk"), P("dp", "blk", None)),
        out_specs=(P("dp", "blk", None), P("dp", "blk", None), P(("blk", "dp"), None)),
        check_vma=False,
    )
```

```python
import functools

import jax
import jax.numpy as jnp
import ml_dtypes
import numpy as np
from jax import lax
from jax.experimental import pallas as pl
from jax.experimental.pallas import tpu as pltpu
from jax.sharding import PartitionSpec as P

MESH = pl.DeviceIdType.MESH
CH = 80
NB = 16
C = CH * NB
TAPS = 9
CELLS = 256
NF = 4
PAD = 768
ROWS = 48
BAND = 320

TREES = [(True, 1), (True, -1), (False, 1), (False, -1)]
BANDS = [0, 1, -1, 2]
CHUNKS = [(0, 256, 4), (256, 384, 3), (640, 256, 3), (896, 384, 4)]


def offsets(tap):
    return tap // 3 - 1, tap % 3 - 1


def moved(v, dy, dx):
    if dy == 0 and dx == 0:
        return v
    cell = lax.broadcasted_iota(jnp.int32, (1, CELLS), 1)
    h = lax.shift_right_logical(cell, 4) + dy
    w = lax.bitwise_and(cell, 15) + dx
    keep = (h >= 0) & (h < 16) & (w >= 0) & (w < 16)
    rolled = pltpu.roll(v, (-(dy * 16 + dx)) % CELLS, axis=1)
    return jnp.where(keep, rolled, jnp.zeros_like(rolled))


def kernel(nz, frames_hbm, weight_hbm, bias_ref, cot_hbm, perm_hbm,
           resp_hbm, fgrad_hbm, wgrad_hbm,
           g, ws, pb, r, rt, perm, cst, csp, resp, fgrad, wgrad,
           pw0, pw1, pw2, pw3, mb0, mb1, mb2, mb3, rp0, rp1, rp2, rp3,
           lsem, wlsem, osem, ag_s, ag_r, w_s, w_r, z_s, z_r, d_s, d_r,
           m_s, m_r, rs_s, rs_r):
    pw, mb, rp = (pw0, pw1, pw2, pw3), (mb0, mb1, mb2, mb3), (rp0, rp1, rp2, rp3)
    dp = lax.axis_index("dp")
    blk = lax.axis_index("blk")
    z, core = dp // 2, lax.rem(dp, 2)
    y, x = blk // 4, lax.rem(blk, 4)
    sib = (z * 2 + 1 - core, blk)

    def plane(b):
        return (dp, b)

    def zdev(step):
        return (lax.rem(z + step + nz, nz) * 2 + core, blk)

    def mine(a, f):
        return g.at[a, f, pl.ds(pl.multiple_of(blk * CH, 16), CH), :]

    loads = {}

    def load(name, src, dst, sem):
        loads[name] = pltpu.make_async_copy(src, dst, sem)
        loads[name].start()

    for a, src in enumerate((frames_hbm, cot_hbm)):
        for f in range(NF):
            load((a, f), src.at[f], mine(a, f), lsem.at[a, f])
    for t in range(TAPS):
        load(t, weight_hbm.at[:, pl.ds(t * C, C)], ws.at[pl.ds(t * CH, CH), :], wlsem.at[t])
    load("perm", perm_hbm, perm, wlsem.at[TAPS])

    barrier = pltpu.get_barrier_semaphore()
    for k in range(1, NB):
        pl.semaphore_signal(barrier, inc=1, device_id=plane(lax.rem(blk + k, NB)), device_id_type=MESH)
    for dev in (sib, zdev(1), zdev(-1)):
        pl.semaphore_signal(barrier, inc=1, device_id=dev, device_id_type=MESH)
    for a in range(2):
        for f in range(NF):
            loads[a, f].wait()
    pl.semaphore_wait(barrier, NB + 2)

    pending = []

    def remote(src, dst, ssem, rsem, dev):
        cp = pltpu.make_async_remote_copy(
            src_ref=src, dst_ref=dst, send_sem=ssem, recv_sem=rsem,
            device_id=dev, device_id_type=MESH)
        cp.start()
        pending.append(cp)

    def wait_for(ref, ssem, rsem):
        pltpu.make_async_remote_copy(
            src_ref=ref, dst_ref=ref, send_sem=ssem, recv_sem=rsem,
            device_id=sib, device_id_type=MESH).wait_recv()

    def at(tree, step_a, step_b):
        first_x, _ = TREES[tree]
        sx, sy = (step_a, step_b) if first_x else (step_b, step_a)
        return lax.rem(y + sy + 4, 4) * 4 + lax.rem(x + sx + 4, 4)

    def block(a, f, ra, rb):
        sgn = TREES[f][1]
        src = at(f, -sgn * (ra if ra < 3 else -1), -sgn * (rb if rb < 3 else -1))
        return g.at[a, f, pl.ds(pl.multiple_of(src * CH, 16), CH), :]

    counts = {}

    def push(a, f, ra, rb, along_a, forward):
        n = counts.get((a, f), 0)
        counts[(a, f)] = n + 1
        sgn = TREES[f][1]
        step = sgn if forward else -sgn
        dev = at(f, step, 0) if along_a else at(f, 0, step)
        if along_a:
            there = (ra + 1 if forward else 3, rb)
        else:
            there = (ra, rb + 1 if forward else 3)
        ref = block(a, f, ra, rb)
        remote(ref, ref, ag_s.at[a, f, n], ag_r.at[a, f, there[0] * 4 + there[1]], plane(dev))

    seen = set()

    def need(a, f, ra, rb):
        if (a, f, ra, rb) in seen or (ra, rb) == (0, 0):
            return
        seen.add((a, f, ra, rb))
        wait_for(block(a, f, ra, rb), ag_s.at[a, f, 0], ag_r.at[a, f, ra * 4 + rb])
        if rb == 0:
            if ra == 1:
                push(a, f, ra, rb, True, True)
            push(a, f, ra, rb, False, True)
            push(a, f, ra, rb, False, False)
        elif rb == 1:
            push(a, f, ra, rb, False, True)

    def events(a, *pairs):
        for ra, rb in pairs:
            for f in range(NF):
                need(a, f, ra, rb)

    def band(a, step):
        for f in range(NF):
            first_x, sgn = TREES[f]
            code = {0: 0, 2: 2, -sgn: 1, sgn: 3}[step]
            for other in (0, 1, 3, 2):
                need(a, f, *((other, code) if first_x else (code, other)))

    def own_sends(a):
        for f in range(NF):
            push(a, f, 0, 0, True, True)
            push(a, f, 0, 0, False, True)
            push(a, f, 0, 0, True, False)
            push(a, f, 0, 0, False, False)

    def band_rows(k):
        return pl.multiple_of(lax.rem(y + BANDS[k] + 4, 4) * BAND, 64)

    def shifted(f):
        cot = mine(1, f)[...].astype(jnp.float32)
        for t in range(TAPS):
            dy, dx = offsets(t)
            cst[t * CH:(t + 1) * CH, :] = moved(cot, -dy, -dx).astype(jnp.bfloat16)
        csp[:, f * CELLS:(f + 1) * CELLS] = jnp.dot(
            perm[...], cst[...], preferred_element_type=jnp.float32).astype(jnp.bfloat16)

    def piece_of(zz, cc):
        d = zz * 2 + cc
        return d // 3, lax.rem(d, 3)

    my_row, my_group = piece_of(z, core)
    row_start = pl.multiple_of(jnp.minimum(my_row, 4) * 16, 16)

    def pack(group):
        for b in range(NB):
            parts = []
            for t in range(TAPS):
                lo, hi = max(t * CH, group * 256), min((t + 1) * CH, (group + 1) * 256)
                if lo < hi:
                    parts.append(ws[pl.ds(pl.multiple_of(t * CH + row_start, 16), 16),
                                    b * CH + lo - t * CH:b * CH + hi - t * CH])
            if group == 2:
                parts.append(jnp.zeros((16, PAD - TAPS * CH), jnp.bfloat16))
            pb[b] = jnp.concatenate(parts, axis=1)

    def send_slices():
        for group in range(3):
            @pl.when(my_group == group)
            def _(group=group):
                pack(group)
        own = pltpu.make_async_copy(pb.at[blk], r.at[blk, my_row, my_group], w_s.at[0])
        own.start()
        for k in range(1, NB):
            b = lax.rem(blk + k, NB)
            remote(pb.at[b], r.at[blk, my_row, my_group], w_s.at[k], w_r.at[k], plane(b))
        return own

    def z_piece(i, k, cc):
        zz = lax.rem(z + (-k if i == 0 else k) + nz, nz)
        row, group = piece_of(zz, cc)
        part = pl.ds(0, NB) if k < 4 else pl.ds(i * 8, 8)
        return r.at[part, row, group]

    def z_push(i, k):
        zz = lax.rem(z + (-k if i == 0 else k) + nz, nz)
        row, group = piece_of(zz, core)
        part = pl.ds(0, NB) if k < 3 else pl.ds(i * 8, 8)
        ref = r.at[part, row, group]
        remote(ref, ref, z_s.at[i, k], z_r.at[i, k + 1], zdev(1 if i == 0 else -1))

    def z_start(own):
        own.wait()
        for k in range(1, NB):
            wait_for(pb.at[0], w_s.at[k], w_r.at[k])
        z_push(0, 0)
        z_push(1, 0)
        ref = r.at[:, my_row, my_group]
        remote(ref, ref, d_s.at[0, 0], d_r.at[0, 0], sib)

    def z_relay(k):
        for i in range(2):
            wait_for(z_piece(i, k, core), z_s.at[i, 0], z_r.at[i, k])
            if k < 4:
                z_push(i, k)
            ref = z_piece(i, k, core)
            remote(ref, ref, d_s.at[i, k], d_r.at[i, k], sib)

    def z_finish():
        for i in range(2):
            for k in range(5):
                if (i, k) != (1, 0):
                    wait_for(z_piece(i, k, 1 - core), d_s.at[0, 0], d_r.at[i, k])

    def turn(group):
        m = jnp.concatenate(
            [r[pl.ds(lax.rem(y + step + 4, 4) * 4, 4), 0:5, group].reshape(BAND, 256) for step in BANDS], axis=0)
        rt[group * 256:(group + 1) * 256, :] = m.T

    def band_slice(a, f, start, size):
        parts = []
        for k in range(4):
            lo, hi = max(start, k * BAND), min(start + size, (k + 1) * BAND)
            if lo < hi:
                parts.append(g[a, f, pl.ds(pl.multiple_of(band_rows(k) + lo - k * BAND, 64), hi - lo), :])
        return parts[0] if len(parts) == 1 else jnp.concatenate(parts, axis=0)

    def wgrad_chunk(q):
        start, size, _ = CHUNKS[q]
        rhs = jnp.concatenate([band_slice(0, f, start, size) for f in range(NF)], axis=1)
        acc = lax.dot_general(csp[...], rhs, (((1,), (1,)), ((), ())), preferred_element_type=jnp.float32)
        for c in range(2):
            pw[q][c] = acc[c * nz * ROWS:(c + 1) * nz * ROWS].reshape(nz, ROWS, size)
        remote(pw[q].at[1 - core], mb[q], m_s.at[q], m_r.at[q], sib)

    def hops(q, i):
        n = CHUNKS[q][2]
        return n if i == 0 else 7 - n

    def rs_wait(q, i, k):
        wait_for(rp[q].at[i, k], rs_s.at[i, q, k], rs_r.at[i, q, k])

    def rs_send(q, i, k):
        if k >= hops(q, i):
            return
        dist = hops(q, i) - k
        to = lax.rem(z + (dist if i == 0 else nz - dist), nz)
        if k > 0:
            rs_wait(q, i, k - 1)
            mb[q][to] = mb[q][to] + rp[q][i, k - 1]
        remote(mb[q].at[to], rp[q].at[i, k], rs_s.at[i, q, k], rs_r.at[i, q, k],
               zdev(1 if i == 0 else -1))

    def rs_start(q):
        wait_for(mb[q], m_s.at[q], m_r.at[q])
        mb[q][...] = mb[q][...] + pw[q][core]
        rs_send(q, 0, 0)
        rs_send(q, 1, 0)

    def rs_round(q, k):
        rs_send(q, 0, k)
        rs_send(q, 1, k)

    def store(vmem, hbm, sem):
        cp = pltpu.make_async_copy(vmem, hbm, sem)
        cp.start()
        loads[len(loads) + 100] = cp

    def convolved(lhs, rhs, sign):
        prod = jnp.dot(lhs[0:TAPS * CH, :], rhs, preferred_element_type=jnp.float32)
        total = None
        for t in range(TAPS):
            dy, dx = offsets(t)
            term = moved(prod[t * CH:(t + 1) * CH], sign * dy, sign * dx)
            total = term if total is None else total + term
        return total

    def respond(f):
        eye = (lax.broadcasted_iota(jnp.int32, (CH, CH), 0) == lax.broadcasted_iota(jnp.int32, (CH, CH), 1))
        column = jnp.sum(jnp.where(eye, bias_ref[...], 0.0), axis=1, keepdims=True)
        resp[f] = (convolved(ws, g[0, f], 1) + column).astype(jnp.bfloat16)

    def grad_of(f):
        fgrad[f] = convolved(rt, band_slice(1, f, 0, C), -1).astype(jnp.bfloat16)

    own_sends(0)
    for t in range(TAPS):
        loads[t].wait()
    own_piece = send_slices()
    loads["perm"].wait()
    shifted(0)
    events(0, (1, 0), (3, 0), (0, 1))
    shifted(1)
    events(0, (2, 0), (0, 2), (0, 3))
    z_start(own_piece)
    shifted(2)
    events(0, (1, 1), (3, 1))
    shifted(3)
    events(0, (2, 1))
    band(0, 0)
    wgrad_chunk(0)
    own_sends(1)
    z_relay(1)
    rs_start(0)
    band(0, 1)
    wgrad_chunk(1)
    events(1, (1, 0), (3, 0), (0, 1))
    z_relay(2)
    band(0, -1)
    wgrad_chunk(2)
    rs_start(1)
    rs_round(0, 1)
    z_relay(3)
    events(1, (2, 0), (0, 2), (0, 3))
    band(0, 2)
    wgrad_chunk(3)
    rs_start(2)
    rs_round(0, 2)
    rs_round(1, 1)
    events(1, (1, 1), (3, 1), (2, 1))
    z_relay(4)
    rs_start(3)
    rs_round(0, 3)
    respond(0)
    rs_round(2, 1)
    rs_round(1, 2)
    respond(1)
    rs_round(3, 1)
    rs_round(2, 2)
    rs_round(1, 3)
    z_finish()
    for group in range(3):
        turn(group)
    rs_round(3, 2)
    rs_round(2, 3)
    respond(2)
    respond(3)
    store(resp, resp_hbm, osem.at[0])
    rs_round(3, 3)
    for step in BANDS:
        band(1, step)
    for f in range(NF):
        grad_of(f)
    store(fgrad, fgrad_hbm, osem.at[1])

    parts = []
    for q in range(len(CHUNKS)):
        for i in range(2):
            rs_wait(q, i, hops(q, i) - 1)
        parts.append(mb[q][z] + rp[q][0, hops(q, 0) - 1] + rp[q][1, hops(q, 1) - 1])
    final = jnp.concatenate(parts, axis=1)
    for case in range(4):
        @pl.when(y == case)
        def _(case=case):
            where = {(case + step) % 4: k for k, step in enumerate(BANDS)}
            ordered = jnp.concatenate(
                [final[:, where[row] * BAND:(where[row] + 1) * BAND] for row in range(4)], axis=1)
            for t in range(TAPS):
                wgrad[:, t * C:(t + 1) * C] = ordered[t * 5:(t + 1) * 5]
    store(wgrad, wgrad_hbm, osem.at[2])

    for cp in pending:
        cp.wait_send()
    for name, cp in loads.items():
        if isinstance(name, int) and name >= 100:
            cp.wait()


def hand_over(a, b, c, a_out, b_out, c_out, a_v, b_v, c_v, sem_in, sem_out):
    trio = ((a, a_v, a_out), (b, b_v, b_out), (c, c_v, c_out))
    ins = [pltpu.make_async_copy(src, v, sem_in.at[i]) for i, (src, v, _) in enumerate(trio)]
    outs = [pltpu.make_async_copy(v, dst, sem_out.at[i]) for i, (_, v, dst) in enumerate(trio)]
    for cp in ins:
        cp.start()
    for one, two in zip(ins, outs):
        one.wait()
        two.start()
    for cp in outs:
        cp.wait()


def solution(mesh):
    nz = mesh.shape["dp"] // 2
    table = np.zeros((PAD, TAPS * CH), np.float32)
    for c in range(2):
        for k in range(nz):
            for t in range(TAPS):
                for j in range(5):
                    table[c * nz * ROWS + k * ROWS + t * 5 + j, t * CH + k * 10 + c * 5 + j] = 1
    table = table.astype(ml_dtypes.bfloat16)

    bf16, f32 = jnp.bfloat16, jnp.float32
    vmem = pl.BlockSpec(memory_space=pltpu.VMEM)
    hbm = pl.BlockSpec(memory_space=pl.ANY)
    dma = pltpu.SemaphoreType.DMA
    nq = len(CHUNKS)
    outs = ((NF, CH, CELLS), bf16), ((NF, CH, CELLS), bf16), ((5, TAPS * C), f32)
    shapes = tuple(jax.ShapeDtypeStruct(*o) for o in outs)

    def body(frames, weight, bias, cotangent):
        results = pl.pallas_call(
            functools.partial(kernel, nz),
            out_shape=shapes,
            in_specs=[hbm, hbm, vmem, hbm, hbm],
            out_specs=(hbm, hbm, hbm),
            scratch_shapes=[
                pltpu.VMEM((2, NF, C, CELLS), bf16),
                pltpu.VMEM((TAPS * CH, C), bf16),
                pltpu.VMEM((NB, 16, 256), bf16),
                pltpu.VMEM((NB, 6, 3, 16, 256), bf16),
                pltpu.VMEM((PAD, C), bf16),
                pltpu.VMEM((PAD, TAPS * CH), bf16),
                pltpu.VMEM((TAPS * CH, CELLS), bf16),
                pltpu.VMEM((PAD, NF * CELLS), bf16),
                *[pltpu.VMEM(*o) for o in outs],
                *[pltpu.VMEM((2, nz, ROWS, n), f32) for _, n, _ in CHUNKS],
                *[pltpu.VMEM((nz, ROWS, n), f32) for _, n, _ in CHUNKS],
                *[pltpu.VMEM((2, 4, ROWS, n), f32) for _, n, _ in CHUNKS],
                dma((2, NF)), dma((TAPS + 1,)), dma((3,)),
                dma((2, NF, 15)), dma((2, NF, 16)),
                dma((NB,)), dma((NB,)),
                dma((2, 4)), dma((2, 5)),
                dma((2, 5)), dma((2, 5)),
                dma((nq,)), dma((nq,)),
                dma((2, nq, 4)), dma((2, nq, 4)),
            ],
            compiler_params=pltpu.CompilerParams(
                collective_id=0, has_side_effects=True, vmem_limit_bytes=60 * 1024 * 1024),
        )(frames, weight, bias.reshape(1, CH), cotangent, jnp.asarray(table))
        return pl.pallas_call(
            hand_over,
            out_shape=shapes,
            in_specs=[hbm] * 3,
            out_specs=(hbm,) * 3,
            scratch_shapes=[*[pltpu.VMEM(*o) for o in outs], dma((3,)), dma((3,))],
        )(*results)

    return jax.shard_map(
        body,
        mesh=mesh,
        in_specs=(P("dp", "blk", None), P("blk", None), P("blk"), P("dp", "blk", None)),
        out_specs=(P("dp", "blk", None), P("dp", "blk", None), P(("blk", "dp"), None)),
        check_vma=False,
    )
```

```python
import functools

import jax
import jax.numpy as jnp
import ml_dtypes
import numpy as np
from jax import lax
from jax.experimental import pallas as pl
from jax.experimental.pallas import tpu as pltpu
from jax.sharding import PartitionSpec as P

MESH = pl.DeviceIdType.MESH
CH = 80
NB = 16
C = CH * NB
TAPS = 9
CELLS = 256
NF = 4
PAD = 768
ROWS = 48

TREES = [(True, 1), (True, -1), (False, 1), (False, -1)]
STEPS = [0, 1, -1, 2]
ARRIVAL = [(0, 0), (1, 0), (2, 0), (0, 1), (0, 2), (3, 0), (0, 3), (1, 1), (1, 2), (2, 1), (2, 2),
           (3, 1), (3, 2), (1, 3), (2, 3), (3, 3)]
CHUNKS = [(0, 384, 4), (384, 384, 3), (768, 256, 3), (1024, 256, 4)]

ORDER = [
    ('wx',), ('own', 0, False), ('own', 0, True), ('block', 0, 1, 0, 1), ('wy',), ('block', 0, 1, 1, 0),
    ('block', 0, 0, 1, 0), ('block', 0, 0, 0, 1), ('block', 0, 3, 3, 0), ('shift', 1), ('block', 0, 0, 3, 0),
    ('block', 0, 2, 3, 0), ('block', 0, 1, 3, 0), ('block', 0, 2, 0, 1), ('shift', 2), ('block', 0, 3, 0, 1),
    ('block', 0, 1, 2, 0), ('block', 0, 3, 0, 3), ('block', 0, 3, 1, 0), ('block', 0, 2, 1, 0), ('own', 1, False),
    ('wz',), ('block', 0, 1, 0, 3), ('block', 0, 2, 0, 3), ('shift', 3), ('own', 1, True), ('shift', 0),
    ('block', 0, 3, 3, 1), ('block', 0, 0, 0, 3), ('block', 0, 0, 1, 3), ('block', 0, 0, 0, 2), ('chunk', 0),
    ('block', 0, 1, 1, 1), ('hop', 1, 1, 0), ('hop', 0, 1, 0), ('block', 0, 1, 2, 3), ('block', 0, 1, 3, 1),
    ('block', 0, 1, 0, 2), ('block', 0, 1, 1, 3), ('hop', 1, 1, 1), ('hop', 0, 1, 1), ('block', 0, 2, 1, 1),
    ('block', 0, 3, 1, 1), ('block', 0, 1, 3, 3), ('block', 0, 2, 3, 3), ('block', 1, 1, 1, 0),
    ('block', 0, 0, 2, 0), ('block', 0, 0, 1, 1), ('block', 0, 3, 0, 2), ('block', 0, 2, 3, 1),
    ('block', 0, 3, 1, 3), ('block', 0, 2, 0, 2), ('block', 0, 2, 2, 0), ('block', 0, 0, 3, 3),
    ('block', 0, 0, 3, 1), ('merge', 0), ('block', 0, 2, 1, 3), ('block', 0, 3, 2, 0), ('chunk', 1),
    ('block', 1, 3, 1, 0), ('hop', 1, 2, 0), ('hop', 0, 2, 0), ('block', 0, 2, 1, 2), ('block', 0, 3, 1, 2),
    ('block', 1, 2, 1, 0), ('block', 0, 3, 3, 2), ('block', 0, 3, 3, 3), ('hop', 1, 2, 1), ('block', 0, 1, 1, 2),
    ('block', 0, 1, 2, 1), ('merge', 1), ('block', 0, 2, 3, 2), ('block', 0, 2, 2, 1), ('hop', 0, 2, 1),
    ('block', 0, 0, 2, 1), ('sum', 0, 0, 1), ('sum', 0, 1, 1), ('block', 0, 0, 2, 3), ('block', 1, 0, 3, 0),
    ('block', 0, 3, 2, 1), ('block', 1, 3, 0, 1), ('block', 1, 0, 1, 0), ('chunk', 2), ('block', 1, 1, 2, 0),
    ('block', 1, 3, 3, 0), ('block', 0, 1, 2, 2), ('block', 0, 0, 1, 2), ('block', 0, 0, 3, 2),
    ('block', 0, 3, 2, 3), ('block', 0, 1, 3, 2), ('block', 1, 2, 2, 0), ('block', 1, 3, 2, 0),
    ('block', 1, 2, 3, 0), ('merge', 2), ('block', 1, 2, 0, 1), ('block', 0, 3, 2, 2), ('block', 0, 2, 2, 2),
    ('block', 0, 2, 2, 3), ('block', 1, 1, 1, 1), ('block', 0, 0, 2, 2), ('chunk', 3), ('block', 1, 0, 2, 0),
    ('sum', 1, 1, 1), ('sum', 1, 0, 1), ('block', 1, 1, 3, 0), ('block', 1, 2, 1, 1), ('resp', 3),
    ('hop', 1, 3, 1), ('block', 1, 3, 1, 1), ('block', 1, 0, 3, 1), ('block', 1, 2, 2, 1), ('block', 1, 1, 2, 1),
    ('block', 1, 3, 3, 1), ('merge', 3), ('block', 1, 1, 0, 1), ('hop', 0, 3, 0), ('block', 1, 0, 0, 1),
    ('block', 1, 0, 1, 1), ('block', 1, 0, 2, 1), ('block', 1, 3, 2, 1), ('block', 1, 1, 3, 1),
    ('block', 1, 2, 3, 1), ('sum', 0, 0, 2), ('hop', 0, 3, 1), ('sum', 2, 1, 1), ('sum', 1, 1, 2),
    ('sum', 3, 0, 1), ('sum', 0, 1, 2), ('sum', 2, 0, 1), ('hop', 1, 3, 0), ('sum', 1, 0, 2), ('hop', 0, 4, 0),
    ('hop', 1, 4, 1), ('sum', 2, 1, 2), ('sum', 3, 1, 1), ('sum', 1, 1, 3), ('sum', 3, 0, 2), ('turn',),
    ('sum', 0, 0, 3), ('sum', 2, 0, 2), ('grad', 1), ('sum', 2, 1, 3), ('grad', 2), ('sum', 3, 1, 2),
    ('sum', 3, 0, 3), ('grad', 3), ('resp', 1), ('resp', 2), ('resp', 0), ('grad', 0),
]


def offsets(tap):
    return tap // 3 - 1, tap % 3 - 1


def moved(v, dy, dx):
    if dy == 0 and dx == 0:
        return v
    cell = lax.broadcasted_iota(jnp.int32, (1, CELLS), 1)
    h = lax.shift_right_logical(cell, 4) + dy
    w = lax.bitwise_and(cell, 15) + dx
    keep = (h >= 0) & (h < 16) & (w >= 0) & (w < 16)
    rolled = pltpu.roll(v, (-(dy * 16 + dx)) % CELLS, axis=1)
    return jnp.where(keep, rolled, jnp.zeros_like(rolled))


def kernel(nz, frames_hbm, weight_hbm, bias_ref, cot_hbm, perm_hbm,
           resp_hbm, fgrad_hbm, wgrad_hbm,
           g, ws, pb, xb, r, rt, perm, cst, csp, resp, fgrad, wgrad, mixed,
           pw0, pw1, pw2, pw3, mb0, mb1, mb2, mb3, rp0, rp1, rp2, rp3,
           lsem, osem, ag_s, ag_r, w_s, w_r, z_s, z_r, d_s, d_r,
           m_s, m_r, rs_s, rs_r):
    pw, mb, rp = (pw0, pw1, pw2, pw3), (mb0, mb1, mb2, mb3), (rp0, rp1, rp2, rp3)
    dp = lax.axis_index("dp")
    blk = lax.axis_index("blk")
    z, core = dp // 2, lax.rem(dp, 2)
    y, x = blk // 4, lax.rem(blk, 4)
    sib = (z * 2 + 1 - core, blk)

    def plane(b):
        return (dp, b)

    def across(sx, sy):
        return lax.rem(y + sy, 4) * 4 + lax.rem(x + sx, 4)

    def zdev(step):
        return (lax.rem(z + step + nz, nz) * 2 + core, blk)

    own_rows = pl.ds(pl.multiple_of(blk * CH, 16), CH)

    loads = {}

    def load(name, src, dst, sem):
        loads[name] = pltpu.make_async_copy(src, dst, sem)
        loads[name].start()

    load("frames", frames_hbm, g.at[0, :, own_rows, :], lsem.at[0])
    load("cot", cot_hbm, g.at[1, :, own_rows, :], lsem.at[1])
    for t in range(TAPS):
        load(t, weight_hbm.at[:, pl.ds(t * C, C)], ws.at[pl.ds(t * CH, CH), :], lsem.at[2])
    load("perm", perm_hbm, perm, lsem.at[3])

    barrier = pltpu.get_barrier_semaphore()
    partners = [plane(across(k, 0)) for k in (1, 2, 3)] + [plane(across(0, k)) for k in (1, 2, 3)]
    for dev in (*partners, sib, zdev(1), zdev(-1)):
        pl.semaphore_signal(barrier, inc=1, device_id=dev, device_id_type=MESH)
    loads["frames"].wait()
    loads["cot"].wait()
    pl.semaphore_wait(barrier, 9)

    def remote(src, dst, ssem, rsem, dev):
        pltpu.make_async_remote_copy(
            src_ref=src, dst_ref=dst, send_sem=ssem, recv_sem=rsem,
            device_id=dev, device_id_type=MESH).start()

    def wait_for(ref, ssem, rsem):
        pltpu.make_async_remote_copy(
            src_ref=ref, dst_ref=ref, send_sem=ssem, recv_sem=rsem,
            device_id=sib, device_id_type=MESH).wait_recv()

    def all_sent(ref, ssem, rsem):
        pltpu.make_async_remote_copy(
            src_ref=ref, dst_ref=ref, send_sem=ssem, recv_sem=rsem,
            device_id=sib, device_id_type=MESH).wait_send()

    def at(tree, step_a, step_b):
        first_x, _ = TREES[tree]
        sx, sy = (step_a, step_b) if first_x else (step_b, step_a)
        return lax.rem(y + sy + 4, 4) * 4 + lax.rem(x + sx + 4, 4)

    def block(a, f, ra, rb):
        sgn = TREES[f][1]
        src = at(f, -sgn * (ra if ra < 3 else -1), -sgn * (rb if rb < 3 else -1))
        return g.at[a, f, pl.ds(pl.multiple_of(src * CH, 16), CH), :]

    def ag_sem(a, f, ra, rb):
        if a == 1 and rb > 1 or a == 1 and (ra, rb) == (0, 3):
            return ag_r.at[1, f, 0]
        return ag_r.at[a, f, ra * 4 + rb]

    def push(a, f, ra, rb, along_a, forward):
        sgn = TREES[f][1]
        step = sgn if forward else -sgn
        dev = at(f, step, 0) if along_a else at(f, 0, step)
        if along_a:
            there = (ra + 1 if forward else 3, rb)
        else:
            there = (ra, rb + 1 if forward else 3)
        ref = block(a, f, ra, rb)
        remote(ref, ref, ag_s.at[a], ag_sem(a, f, *there), plane(dev))

    def block_task(a, f, ra, rb):
        wait_for(block(a, f, ra, rb), ag_s.at[a], ag_sem(a, f, ra, rb))
        if rb == 0:
            if ra == 1:
                push(a, f, ra, rb, True, True)
            push(a, f, ra, rb, False, True)
            push(a, f, ra, rb, False, False)
        elif rb == 1:
            push(a, f, ra, rb, False, True)

    def own_sends(a, along_x):
        for forward in (True, False):
            for f in range(NF):
                push(a, f, 0, 0, TREES[f][0] == along_x, forward)

    def shifted(f):
        if "perm" in loads:
            loads.pop("perm").wait()
        cot = g[1, f, own_rows, :].astype(jnp.float32)
        for t in range(TAPS):
            dy, dx = offsets(t)
            cst[t * CH:(t + 1) * CH, :] = moved(cot, -dy, -dx).astype(jnp.bfloat16)
        csp[:, f * CELLS:(f + 1) * CELLS] = jnp.dot(
            perm[...], cst[...], preferred_element_type=jnp.float32).astype(jnp.bfloat16)

    def piece_of(zz, cc):
        d = zz * 2 + cc
        return d // 3, lax.rem(d, 3)

    my_row, my_group = piece_of(z, core)
    row_start = pl.multiple_of(jnp.minimum(my_row, 4) * 16, 16)

    def pack(group):
        for b in range(NB):
            parts = []
            for t in range(TAPS):
                lo, hi = max(t * CH, group * 256), min((t + 1) * CH, (group + 1) * 256)
                if lo < hi:
                    parts.append(ws[pl.ds(pl.multiple_of(t * CH + row_start, 16), 16),
                                    b * CH + lo - t * CH:b * CH + hi - t * CH])
            if group == 2:
                parts.append(jnp.zeros((16, PAD - TAPS * CH), jnp.bfloat16))
            pb[b % 4, b // 4] = jnp.concatenate(parts, axis=1)

    def slices_along_x():
        pltpu.make_async_copy(ws, ws, lsem.at[2]).wait()
        for group in range(3):
            @pl.when(my_group == group)
            def _(group=group):
                pack(group)
        load("x", pb.at[x], xb.at[x], lsem.at[4])
        for k in (1, 3, 2):
            remote(pb.at[lax.rem(x + k, 4)], xb.at[x], w_s.at[0], w_r.at[0], plane(across(k, 0)))

    def slices_along_y():
        loads["x"].wait()
        wait_for(xb.at[pl.ds(0, 3)], w_s.at[0], w_r.at[0])
        here = r.at[pl.ds(y * 4, 4), my_row, my_group]
        load("y", xb.at[:, y], here, lsem.at[5])
        for k in (1, 3, 2):
            remote(xb.at[:, lax.rem(y + k, 4)], here, w_s.at[1], w_r.at[1], plane(across(0, k)))

    def z_piece(i, k, h, cc):
        zz = lax.rem(z + (-k if i == 0 else k) + nz, nz)
        row, group = piece_of(zz, cc)
        return r.at[pl.ds(h * 8, 8), row, group]

    def z_push(i, k, h):
        ref = z_piece(i, k, h, core)
        remote(ref, ref, z_s.at[0], z_r.at[i, k, h], zdev(1 if i == 0 else -1))

    def to_sibling(i, k, h):
        ref = z_piece(i, k, h, core)
        remote(ref, ref, d_s.at[0], d_r.at[0], sib)

    def slices_along_z():
        loads["y"].wait()
        wait_for(xb.at[pl.ds(0, 3)], w_s.at[1], w_r.at[1])
        for h in range(2):
            z_push(0, 0, h)
            z_push(1, 0, h)
        for h in range(2):
            to_sibling(0, 0, h)

    def z_task(i, k, h):
        wait_for(z_piece(i, k, h, core), z_s.at[0], z_r.at[i, k - 1, h])
        if k < 3 or (k == 3 and h == i):
            z_push(i, k, h)
        to_sibling(i, k, h)

    def slices_done():
        wait_for(r.at[:, 0:4, 0:2], d_s.at[0], d_r.at[0])
        for group in range(3):
            turn(group)

    def turn(group):
        m = r[:, 0:5, group].reshape(C, 256)
        rt[group * 256:(group + 1) * 256, :] = m.T

    def arrived_rows(f, start, size):
        parts = []
        for n, (kx, ky) in enumerate(ARRIVAL):
            lo, hi = max(start, n * CH), min(start + size, (n + 1) * CH)
            if lo < hi:
                src = lax.rem(y + STEPS[ky] + 4, 4) * 4 + lax.rem(x + STEPS[kx] + 4, 4)
                parts.append(g[0, f, pl.ds(pl.multiple_of(src * CH + lo - n * CH, 16), hi - lo), :])
        return jnp.concatenate(parts, axis=0)

    def wgrad_chunk(q):
        start, size, _ = CHUNKS[q]
        rhs = jnp.concatenate([arrived_rows(f, start, size) for f in range(NF)], axis=1)
        acc = lax.dot_general(csp[...], rhs, (((1,), (1,)), ((), ())), preferred_element_type=jnp.float32)
        for c in range(2):
            pw[q][c] = acc[c * nz * ROWS:(c + 1) * nz * ROWS].reshape(nz, ROWS, size)
        remote(pw[q].at[1 - core], mb[q], m_s.at[q], m_r.at[q], sib)

    def hops(q, i):
        n = CHUNKS[q][2]
        return n if i == 0 else 7 - n

    def rs_wait(q, i, k):
        wait_for(rp[q].at[i, k], rs_s.at[q], rs_r.at[i, q, k])

    def rs_send(q, i, k):
        if k >= hops(q, i):
            return
        dist = hops(q, i) - k
        to = lax.rem(z + (dist if i == 0 else nz - dist), nz)
        if k > 0:
            rs_wait(q, i, k - 1)
            mb[q][to] = mb[q][to] + rp[q][i, k - 1]
        remote(mb[q].at[to], rp[q].at[i, k], rs_s.at[q], rs_r.at[i, q, k],
               zdev(1 if i == 0 else -1))

    def rs_start(q):
        wait_for(mb[q], m_s.at[q], m_r.at[q])
        mb[q][...] = mb[q][...] + pw[q][core]
        rs_send(q, 0, 0)
        rs_send(q, 1, 0)

    def store(vmem, hbm, sem):
        cp = pltpu.make_async_copy(vmem, hbm, sem)
        cp.start()
        loads[len(loads) + 100] = cp

    def convolved(lhs, rhs, sign):
        prod = jnp.dot(lhs[0:TAPS * CH, :], rhs, preferred_element_type=jnp.float32)
        total = None
        for t in range(TAPS):
            dy, dx = offsets(t)
            term = moved(prod[t * CH:(t + 1) * CH], sign * dy, sign * dx)
            total = term if total is None else total + term
        return total

    def respond(f):
        eye = (lax.broadcasted_iota(jnp.int32, (CH, CH), 0) == lax.broadcasted_iota(jnp.int32, (CH, CH), 1))
        column = jnp.sum(jnp.where(eye, bias_ref[...], 0.0), axis=1, keepdims=True)
        resp[f] = (convolved(ws, g[0, f], 1) + column).astype(jnp.bfloat16)

    def grad_of(f):
        wait_for(g.at[1, f, pl.ds(0, 8 * CH), :], ag_s.at[1], ag_r.at[1, f, 0])
        fgrad[f] = convolved(rt, g[1, f], -1).astype(jnp.bfloat16)

    tasks = {
        "own": own_sends, "block": block_task, "shift": shifted, "chunk": wgrad_chunk,
        "merge": rs_start, "sum": rs_send, "resp": respond, "grad": grad_of,
        "wx": slices_along_x, "wy": slices_along_y, "wz": slices_along_z,
        "hop": z_task, "turn": slices_done,
    }
    for name, *rest in ORDER:
        tasks[name](*rest)
    store(resp, resp_hbm, osem.at[0])
    store(fgrad, fgrad_hbm, osem.at[1])

    parts = []
    for q in range(len(CHUNKS)):
        for i in range(2):
            rs_wait(q, i, hops(q, i) - 1)
        parts.append(mb[q][z] + rp[q][0, hops(q, 0) - 1] + rp[q][1, hops(q, 1) - 1])
    final = jnp.concatenate(parts, axis=1)
    place = {block: n for n, block in enumerate(ARRIVAL)}
    for case in range(4):
        where = {(case + step) % 4: k for k, step in enumerate(STEPS)}

        @pl.when(x == case)
        def _(where=where):
            pieces = [place[where[col], ky] for ky in range(4) for col in range(4)]
            mixed[...] = jnp.concatenate([final[:, n * CH:(n + 1) * CH] for n in pieces], axis=1)

    for case in range(4):
        where = {(case + step) % 4: k for k, step in enumerate(STEPS)}

        @pl.when(y == case)
        def _(where=where):
            bands = [where[row] * 4 * CH for row in range(4)]
            ordered = jnp.concatenate([mixed[:, n:n + 4 * CH] for n in bands], axis=1)
            for t in range(TAPS):
                wgrad[:, t * C:(t + 1) * C] = ordered[t * 5:(t + 1) * 5]
    store(wgrad, wgrad_hbm, osem.at[2])

    for a in range(2):
        all_sent(g.at[a, :, pl.ds(0, 15 * CH), :], ag_s.at[a], ag_r.at[a, 0, 1])
        all_sent(xb.at[pl.ds(0, 3)], w_s.at[a], w_r.at[a])
    all_sent(r.at[pl.ds(0, 14), 0:4, 0:2], z_s.at[0], z_r.at[0, 0, 0])
    all_sent(r.at[:, 0:4, 0:2], d_s.at[0], d_r.at[0])
    for q in range(len(CHUNKS)):
        all_sent(mb[q], m_s.at[q], m_r.at[q])
        all_sent(mb[q].at[pl.ds(0, nz - 1)], rs_s.at[q], rs_r.at[0, q, 0])
    for name, cp in loads.items():
        if isinstance(name, int) and name >= 100:
            cp.wait()


def hand_over(a, b, c, a_out, b_out, c_out, a_v, b_v, c_v, sem_in, sem_out):
    trio = ((a, a_v, a_out), (b, b_v, b_out), (c, c_v, c_out))
    ins = [pltpu.make_async_copy(src, v, sem_in.at[i]) for i, (src, v, _) in enumerate(trio)]
    outs = [pltpu.make_async_copy(v, dst, sem_out.at[i]) for i, (_, v, dst) in enumerate(trio)]
    for cp in ins:
        cp.start()
    for one, two in zip(ins, outs):
        one.wait()
        two.start()
    for cp in outs:
        cp.wait()


def solution(mesh):
    nz = mesh.shape["dp"] // 2
    table = np.zeros((PAD, TAPS * CH), np.float32)
    for c in range(2):
        for k in range(nz):
            for t in range(TAPS):
                for j in range(5):
                    table[c * nz * ROWS + k * ROWS + t * 5 + j, t * CH + k * 10 + c * 5 + j] = 1
    table = table.astype(ml_dtypes.bfloat16)

    bf16, f32 = jnp.bfloat16, jnp.float32
    vmem = pl.BlockSpec(memory_space=pltpu.VMEM)
    hbm = pl.BlockSpec(memory_space=pl.ANY)
    dma = pltpu.SemaphoreType.DMA
    nq = len(CHUNKS)
    outs = ((NF, CH, CELLS), bf16), ((NF, CH, CELLS), bf16), ((5, TAPS * C), f32)
    shapes = tuple(jax.ShapeDtypeStruct(*o) for o in outs)

    def body(frames, weight, bias, cotangent):
        results = pl.pallas_call(
            functools.partial(kernel, nz),
            out_shape=shapes,
            in_specs=[hbm, hbm, vmem, hbm, hbm],
            out_specs=(hbm, hbm, hbm),
            scratch_shapes=[
                pltpu.VMEM((2, NF, C, CELLS), bf16),
                pltpu.VMEM((TAPS * CH, C), bf16),
                pltpu.VMEM((4, 4, 16, 256), bf16),
                pltpu.VMEM((4, 4, 16, 256), bf16),
                pltpu.VMEM((NB, 6, 3, 16, 256), bf16),
                pltpu.VMEM((PAD, C), bf16),
                pltpu.VMEM((PAD, TAPS * CH), bf16),
                pltpu.VMEM((TAPS * CH, CELLS), bf16),
                pltpu.VMEM((PAD, NF * CELLS), bf16),
                *[pltpu.VMEM(*o) for o in outs],
                pltpu.VMEM((ROWS, C), f32),
                *[pltpu.VMEM((2, nz, ROWS, n), f32) for _, n, _ in CHUNKS],
                *[pltpu.VMEM((nz, ROWS, n), f32) for _, n, _ in CHUNKS],
                *[pltpu.VMEM((2, 4, ROWS, n), f32) for _, n, _ in CHUNKS],
                dma((6,)), dma((3,)),
                dma((2,)), dma((2, NF, 16)),
                dma((2,)), dma((2,)),
                dma((1,)), dma((2, 4, 2)),
                dma((1,)), dma((1,)),
                dma((nq,)), dma((nq,)),
                dma((nq,)), dma((2, nq, 4)),
            ],
            compiler_params=pltpu.CompilerParams(
                collective_id=0, has_side_effects=True, vmem_limit_bytes=60 * 1024 * 1024),
        )(frames, weight, bias.reshape(1, CH), cotangent, jnp.asarray(table))
        return pl.pallas_call(
            hand_over,
            out_shape=shapes,
            in_specs=[hbm] * 3,
            out_specs=(hbm,) * 3,
            scratch_shapes=[*[pltpu.VMEM(*o) for o in outs], dma((3,)), dma((3,))],
        )(*results)

    return jax.shard_map(
        body,
        mesh=mesh,
        in_specs=(P("dp", "blk", None), P("blk", None), P("blk"), P("dp", "blk", None)),
        out_specs=(P("dp", "blk", None), P("dp", "blk", None), P(("blk", "dp"), None)),
        check_vma=False,
    )
```
